32 devices in a mesh: dp: 4 (over z), tensor: 2 (over core), section: 4 (over y, x).
Axes of the slice: x: 2, y: 2, z: 4, core: 2. Of those that a mesh axis runs over, the one named last changes fastest.
Arguments:
- grads: bfloat16 [4, 2, 4096, 1024], P('dp', None, 'section', 'tensor'), may hold values from -144 to 144
- errors: float32 [4, 2, 4096, 1024], P('dp', None, 'section', 'tensor'), may hold values from -3 to 3
- start_q: float32 [2, 32, 1024], P(None, None, 'tensor'), may hold values from -6 to 6
- master: float32 [2, 4, 1024, 1024], P(None, 'section', 'dp', 'tensor'), may hold values from -6 to 6
- momentum: float32 [2, 4, 1024, 1024], P(None, 'section', 'dp', 'tensor'), may hold values from -1.2 to 1.2
- gain_grads: float32 [4, 2, 4096], P('dp'), may hold values from -6 to 6
- gain_master: float32 [2, 4096], P(None, 'dp'), may hold values from 0.5 to 1.5
- gain_momentum: float32 [2, 4096], P(None, 'dp'), may hold values from -1.2 to 1.2
Outputs:
- new_errors: float32 [4, 2, 4096, 1024], P('dp', None, 'section', 'tensor')
- new_momentum: float32 [2, 4, 1024, 1024], P(None, 'section', 'dp', 'tensor')
- new_master: float32 [2, 4, 1024, 1024], P(None, 'section', 'dp', 'tensor')
- weights: bfloat16 [2, 4096, 1024], P(None, 'section', 'tensor')
- new_gain_momentum: float32 [2, 4096], P(None, 'dp')
- new_gain_master: float32 [2, 4096], P(None, 'dp')
- gains: bfloat16 [2, 4096], replicated
The draws below stay inside these ranges and needn't reach their ends.
All inputs are finite; a program needn't handle non-finite values.
Results may differ from the reference program's by a relative error of at most 0.0004.
Values may be sent and summed in bfloat16 or wider, within the bound.
A program may use at most 64 MiB of HBM per device.

```python
import math
import jax
import jax.numpy as jnp
from jax import lax

D = 4096
KVW = 1024
RANK = 32
ROUNDS = 2
N_DP = 4
N_SECTION = 4


def draw_grads(key, part):
    key_rows, key_cols, key_order, key_base = jax.random.split(jax.random.fold_in(key, 71), 4)
    shape = (N_DP, 2, D, KVW)
    places = jnp.arange(D, dtype=jnp.float32)
    rising = 1.0 + 2.0 * places / (D - 1)
    row_scale = rising[None, :] * jnp.exp(jax.random.uniform(key_rows, (2, D), jnp.float32) * math.log(4.0))
    col_scale = jnp.exp(jax.random.uniform(key_cols, (2, KVW), jnp.float32) * math.log(3.0))
    order = jax.random.permutation(key_order, N_DP)
    blocks = jnp.arange(D, dtype=jnp.int32) // (D // N_DP)
    spiked = jnp.where(blocks[None, :] == order[:, None], 4.0, 1.0).astype(jnp.float32)
    base = jnp.clip(jax.random.normal(key_base, shape, jnp.float32), -6.0, 6.0)
    values = base * spiked[:, None, :, None] * row_scale[None, :, :, None] * col_scale[None, :, None, :]
    return (values / 6.0).astype(jnp.bfloat16)


def with_spikes(values, key, source, target, parts, factor):
    def block_of(position):
        return (jnp.arange(values.shape[position]) // (values.shape[position] // parts)).reshape((-1,) + (1,) * (values.ndim - 1 - position))

    near = jax.random.permutation(key, parts)[block_of(target)]
    other_side = (block_of(target) + parts // 2) % parts
    return jnp.where((block_of(source) == near) | (block_of(source) == other_side), factor * values, values)


def steps_of(key, extent, pieces, smallest, top_value):
    def one(axis_at, shards_of):
        draws = jax.random.uniform(jax.random.fold_in(jax.random.fold_in(key, 6), axis_at), (shards_of,), jnp.float32, smallest / len(pieces), top_value / len(pieces))
        return jnp.repeat(jnp.exp(draws), extent[axis_at] // shards_of).reshape((-1,) + (1,) * (len(extent) - axis_at - 1))

    loudness = one(*pieces[0])
    for cut in pieces[1:]:
        loudness = loudness * one(*cut)
    return loudness


def scatter_about(stream_key, shape, spread, reach, shards=(), kind=jnp.bfloat16):
    loudness = steps_of(stream_key, shape, shards, -0.22, 0.18) if shards else 1.0
    entries = jax.random.normal(stream_key, shape, jnp.float32) * spread * loudness
    return jnp.minimum(jnp.maximum(entries, -reach), reach).astype(kind)


def noise_with(own_key, shape, width, bound, pieces, heavy, kind=jnp.bfloat16):
    values = width * jax.random.normal(own_key, shape, jnp.float32)
    if pieces:
        values = values * steps_of(own_key, shape, pieces, -0.22, 0.18)
    return jnp.clip(with_spikes(values, jax.random.fold_in(own_key, 3), *heavy), -bound, bound).astype(kind)


def setup_inputs(seed: int = 0) -> dict:
    key_list = jax.random.split(jax.random.key(seed), 9)
    return {
        "grads": draw_grads(jax.random.fold_in(key_list[8], 71), 0),
        "errors": scatter_about(key_list[1], (N_DP, 2, D, KVW), 0.5, 3.0, ((0, 4), (2, 4), (3, 2)), jnp.float32),
        "start_q": scatter_about(key_list[2], (2, RANK, KVW), 1.0, 6.0, ((2, 2),), jnp.float32),
        "master": scatter_about(key_list[3], (2, N_SECTION, D // N_SECTION, KVW), 1.0, 6.0, ((1, 4), (2, 4), (3, 2)), jnp.float32),
        "momentum": scatter_about(key_list[4], (2, N_SECTION, D // N_SECTION, KVW), 0.2, 1.2, ((1, 4), (2, 4), (3, 2)), jnp.float32),
        "gain_grads": noise_with(key_list[5], (N_DP, 2, D), 1.0, 6.0, ((0, 4),), (0, 2, 4, 2.0), jnp.float32),
        "gain_master": jnp.clip(1.0 + 0.1 * jax.random.normal(key_list[6], (2, D), jnp.float32), 0.5, 1.5),
        "gain_momentum": scatter_about(key_list[7], (2, D), 0.2, 1.2, ((1, 4),), jnp.float32),
    }


beta_decay = 0.9
step_rate = 0.25

def reference(grads, errors, start_q, master, momentum, gain_grads, gain_master, gain_momentum):
    highest = lax.Precision.HIGHEST

    def left_mean(right_factor):

        def accumulate(total, pair):
            grad_one, error_one = pair
            merged = grad_one.astype(jnp.float32) + error_one
            return (total + jnp.einsum('jak,jrk->jra', merged, right_factor, precision=highest), None)
        total, _ = lax.scan(accumulate, jnp.zeros((2, RANK, D), jnp.float32), (grads, errors))
        return total / N_DP

    def right_mean(left_factor):

        def accumulate(total, pair):
            grad_one, error_one = pair
            merged = grad_one.astype(jnp.float32) + error_one
            return (total + jnp.einsum('jak,jra->jrk', merged, left_factor, precision=highest), None)
        total, _ = lax.scan(accumulate, jnp.zeros((2, RANK, KVW), jnp.float32), (grads, errors))
        return total / N_DP

    def orthonormal(left_factor):
        gram = jnp.einsum('jra,jsa->jrs', left_factor, left_factor, precision=highest)
        lower = jnp.linalg.cholesky(gram)
        return jax.vmap(lambda tri, rhs: jax.scipy.linalg.solve_triangular(tri, rhs, lower=True))(lower, left_factor)
    right_factor = start_q
    for turn in range(ROUNDS):
        left_hat = orthonormal(left_mean(right_factor))
        right_factor = right_mean(left_hat)
    approx = jnp.einsum('jra,jrk->jak', left_hat, right_factor, precision=highest)
    new_errors = grads.astype(jnp.float32) + errors - approx[None]
    update = approx.reshape(2, N_SECTION, D // N_SECTION, KVW)
    new_momentum = beta_decay * momentum + update
    new_master = master - step_rate * new_momentum
    weights = new_master.astype(jnp.bfloat16).reshape(2, D, KVW)
    gain_mean = jnp.sum(gain_grads, axis=0) / N_DP
    new_gain_momentum = beta_decay * gain_momentum + gain_mean
    new_gain_master = gain_master - step_rate * new_gain_momentum
    gains = new_gain_master.astype(jnp.bfloat16)
    return (new_errors, new_momentum, new_master, weights, new_gain_momentum, new_gain_master, gains)
```

```python
import functools

import jax
import jax.numpy as jnp
from jax import lax
from jax.experimental import pallas as pl
from jax.experimental.pallas import tpu as pltpu
from jax.sharding import PartitionSpec as P

ROUNDS = 2


beta_decay = 0.9
step_rate = 0.25

MESH = pl.DeviceIdType.MESH
F32 = jnp.float32
BF16 = jnp.bfloat16
NN = (((1,), (0,)), ((), ()))
NT = (((1,), (1,)), ((), ()))
TN = (((0,), (0,)), ((), ()))


def local_plain(grads, errors, start_q, master, momentum, gain_grads, gain_master, gain_momentum):
    highest = lax.Precision.HIGHEST
    replicas = lax.axis_size("dp")
    merged = grads[0].astype(jnp.float32) + errors[0]
    right_factor = start_q
    for turn in range(ROUNDS):
        partial_left = jnp.einsum("jak,jrk->jra", merged, right_factor, precision=highest)
        reduce_summed = lax.psum(partial_left, ("dp", "tensor"))
        left_factor = reduce_summed / replicas
        gram_part = jnp.einsum("jra,jsa->jrs", left_factor, left_factor, precision=highest)
        gram = lax.psum(gram_part, "section")
        lower = jnp.linalg.cholesky(gram)
        left_hat = jax.vmap(
            lambda tri, rhs: jax.scipy.linalg.solve_triangular(tri, rhs, lower=True)
        )(lower, left_factor)
        partial_right = jnp.einsum("jak,jra->jrk", merged, left_hat, precision=highest)
        summed = lax.psum(partial_right, ("dp", "section"))
        right_factor = summed / replicas
    approx = jnp.einsum("jra,jrk->jak", left_hat, right_factor, precision=highest)
    new_errors = (merged - approx)[None]
    share_rows = approx.shape[1] // replicas
    row_start = lax.axis_index("dp") * share_rows
    share = lax.dynamic_slice_in_dim(approx, row_start, share_rows, 1)[:, None]
    new_momentum = beta_decay * momentum + share
    new_master = master - step_rate * new_momentum
    gain_sum_all = lax.psum(gain_grads[0], "dp")
    share_width = gain_sum_all.shape[1] // replicas
    gain_share = lax.dynamic_slice_in_dim(
        gain_sum_all, lax.axis_index("dp") * share_width, share_width, 1
    )
    gain_mean = gain_share / replicas
    new_gain_momentum = beta_decay * gain_momentum + gain_mean
    new_gain_master = gain_master - step_rate * new_gain_momentum
    gathered, gains = (
        lax.all_gather(new_master.astype(jnp.bfloat16), "dp", axis=2, tiled=True),
        lax.all_gather(new_gain_master.astype(jnp.bfloat16), "dp", axis=1, tiled=True),
    )
    weights = gathered.reshape(gathered.shape[0], gathered.shape[2], gathered.shape[3])
    return (
        new_errors,
        new_momentum,
        new_master,
        weights,
        new_gain_momentum,
        new_gain_master,
        gains,
    )


def pieces(x):
    high = x.astype(BF16)
    rest = x - high.astype(F32)
    mid = rest.astype(BF16)
    return high, mid, (rest - mid.astype(F32)).astype(BF16)


def dot(a, b, dims):
    return lax.dot_general(a, b, dims, preferred_element_type=F32)


def exact(a, b, dims):
    return lax.dot_general(a, b, dims, precision=lax.Precision.HIGHEST, preferred_element_type=F32)


def folded(by_high, by_low, rank):
    small = by_high[2 * rank :] + by_low[rank : 2 * rank]
    return by_high[:rank] + ((by_high[rank : 2 * rank] + by_low[:rank]) + small)


def eliminate(table, first, last, rows):
    for i in range(first, last):
        row = table[:, i : i + 1, :]
        column = table[:, :, i : i + 1]
        scaled = row * (1.0 / table[:, i : i + 1, i : i + 1])
        table = table - jnp.where(rows > i, column, 0.0) * scaled
    return table


def kernel(
    nd, ns, early,
    grads, errors, start_q, master, momentum, gain_grads, gain_master, gain_momentum,
    err_out, mom_out, master_out, w_out, gmom_out, gmaster_out, gains_out,
    gbuf, ebuf, mhi, mlo, mabuf, mobuf,
    ppart, from_core, psum, from_z, pfull,
    gram, upart, from_s, zsum, usum, ufull,
    cbuf, wearly, wlate, gain_in, gain_all, left_stack, right_stack,
    in_sem, out_sem, s_core, r_core, s_z, r_z, s_gz, r_gz, s_fw, r_fw,
    s_gr, r_gr, s_u, r_u, s_uz, r_uz, s_ug, r_ug, s_c, r_c, s_w, r_w, s_g1, r_g1, s_g2, r_g2,
):
    rank, rows = start_q.shape[1], errors.shape[1]
    share = rows // nd
    late = share - early
    piece = rank // nd
    slab = 2 * rank // ns
    width = gain_master.shape[1]
    dp, me, sec = lax.axis_index("dp"), lax.axis_index("tensor"), lax.axis_index("section")
    sib = 1 - me

    def at_z(k):
        return lax.rem(dp + k, nd)

    def from_at_z(k):
        return lax.rem(dp + nd - k, nd)

    def at_s(k):
        return lax.rem(sec + k, ns)

    def from_at_s(k):
        return lax.rem(sec + ns - k, ns)

    def remote(src, dst, send, recv, where):
        return pltpu.make_async_remote_copy(
            src_ref=src, dst_ref=dst, send_sem=send, recv_sem=recv, device_id=where, device_id_type=MESH
        )

    def load(j, slot):
        return (
            pltpu.make_async_copy(grads.at[j], gbuf.at[j], in_sem.at[2 * slot]),
            pltpu.make_async_copy(errors.at[j], ebuf.at[j], in_sem.at[2 * slot + 1]),
        )

    for slot, j in enumerate((sib, me)):
        for copy in load(j, slot):
            copy.start()
    load_master = pltpu.make_async_copy(master, mabuf, in_sem.at[4])
    load_momentum = pltpu.make_async_copy(momentum, mobuf, in_sem.at[5])
    load_master.start()
    load_momentum.start()

    barrier = pltpu.get_barrier_semaphore()
    pl.semaphore_signal(barrier, inc=1, device_id={"tensor": sib}, device_id_type=MESH)
    for k in range(1, nd):
        pl.semaphore_signal(barrier, inc=1, device_id={"dp": at_z(k)}, device_id_type=MESH)
    for k in range(1, ns):
        pl.semaphore_signal(barrier, inc=1, device_id={"section": at_s(k)}, device_id_type=MESH)

    sends = []

    def prepare(j, slot):
        for copy in load(j, slot):
            copy.wait()
        stack = jnp.concatenate(pieces(start_q[j]), axis=0)

        def chunk(i, carry):
            base = pl.multiple_of(i * 256, 256)
            for sub in range(4):
                at = pl.ds(pl.multiple_of(base + sub * 64, 64), 64)
                merged = gbuf[j, at, :].astype(F32) + ebuf[j, at, :]
                ebuf[j, at, :] = merged
                high = merged.astype(BF16)
                mhi[j, at, :] = high
                mlo[j, at, :] = (merged - high.astype(F32)).astype(BF16)
            at = pl.ds(base, 256)
            ppart[0, j, :, at] = folded(
                dot(stack, mhi[j, at, :], NT), dot(stack[: 2 * rank], mlo[j, at, :], NT), rank
            )
            return carry

        lax.fori_loop(0, rows // 256, chunk, 0)

    def left_part(turn, j, factor):
        stack = jnp.concatenate(pieces(factor), axis=0)
        ppart[turn, j] = folded(dot(stack, mhi[j], NT), dot(stack[: 2 * rank], mlo[j], NT), rank)

    lanes = lax.broadcasted_iota(jnp.int32, (2, rank, 128), 2)
    sub_rows = lax.broadcasted_iota(jnp.int32, (2, rank, 128), 1)
    unit = jnp.where(lanes == sub_rows + rank, 1.0, 0.0).astype(F32)
    row_of = lax.broadcasted_iota(jnp.int32, (2, rank, 1), 1)
    gain_copies = []
    c_copies = []
    factors = None
    for turn in range(ROUNDS):
        if turn == 0:
            prepare(sib, 0)
            pl.semaphore_wait(barrier, nd + ns - 1)
        else:
            for j in range(2):
                left_part(turn, j, factors[j])
        swap = remote(
            ppart.at[turn, sib], from_core.at[turn], s_core.at[turn], r_core.at[turn], {"tensor": sib}
        )
        swap.start()
        if turn == 0:
            prepare(me, 1)
        swap.wait()
        psum[turn] = ppart[turn, me] + from_core[turn]
        copies = []
        for k in range(1, nd):
            to = at_z(k)
            copy = remote(
                psum.at[turn, pl.ds(pl.multiple_of(to * piece, piece), piece), :],
                from_z.at[turn, k - 1],
                s_z.at[turn, k - 1],
                r_z.at[turn, k - 1],
                {"dp": to},
            )
            copy.start()
            copies.append(copy)
        mine = pl.ds(pl.multiple_of(dp * piece, piece), piece)
        if turn == 0:
            load_master.wait()
            load_momentum.wait()
            for j in range(2):
                at = pl.ds(0, early)
                cbuf[dp, j] = mabuf[j, at, :] - (step_rate * beta_decay) * mobuf[j, at, :]
        for copy in copies:
            copy.wait()
        total = psum[turn, mine, :]
        for k in range(1, nd):
            total = total + from_z[turn, k - 1]
        pfull[turn, me, mine, :] = total * (1.0 / nd)
        own = pfull.at[turn, me, mine, :]
        gathers = []
        for k in range(1, nd):
            copy = remote(own, own, s_gz.at[turn, k - 1], r_gz.at[turn, k - 1], {"dp": at_z(k)})
            copy.start()
            gathers.append(copy)
        copy = remote(own, own, s_fw.at[turn, 0], r_fw.at[turn, 0], {"tensor": sib})
        copy.start()
        forwards = [copy]
        for k in range(1, nd):
            there = pl.ds(pl.multiple_of(from_at_z(k) * piece, piece), piece)
            block = pfull.at[turn, me, there, :]
            remote(block, block, s_gz.at[turn, k - 1], r_gz.at[turn, k - 1], {"dp": at_z(k)}).wait_recv()
            copy = remote(block, block, s_fw.at[turn, k], r_fw.at[turn, k], {"tensor": sib})
            copy.start()
            forwards.append(copy)
        for k in range(nd):
            there = pl.ds(pl.multiple_of(from_at_z(k) * piece, piece), piece)
            block = pfull.at[turn, sib, there, :]
            remote(block, block, s_fw.at[turn, k], r_fw.at[turn, k], {"tensor": sib}).wait_recv()
        sends += gathers + forwards

        for j in range(2):
            left = pfull[turn, j]
            gram[turn, sec, j] = jnp.concatenate(
                [exact(left, left, NT), jnp.zeros((rank, 128 - rank), F32)], axis=1
            )
        grams = []
        for k in range(1, ns):
            copy = remote(
                gram.at[turn, sec], gram.at[turn, sec], s_gr.at[turn, k - 1], r_gr.at[turn, k - 1],
                {"section": at_s(k)},
            )
            copy.start()
            grams.append(copy)
        sends += grams
        for j in range(2):
            stack = jnp.concatenate(pieces(pfull[turn, j]), axis=0)
            upart[turn, pl.ds(j * rank, rank), :] = folded(
                dot(stack, mhi[j], NN), dot(stack[: 2 * rank], mlo[j], NN), rank
            )
        copies = []
        for k in range(1, ns):
            to = at_s(k)
            copy = remote(
                upart.at[turn, pl.ds(pl.multiple_of(to * slab, slab), slab), :],
                from_s.at[turn, k - 1],
                s_u.at[turn, k - 1],
                r_u.at[turn, k - 1],
                {"section": to},
            )
            copy.start()
            copies.append(copy)
        if turn == 0:
            for k in range(1, nd):
                to = at_z(k)
                copy = remote(
                    gain_grads.at[:, pl.ds(pl.multiple_of(to * width, width), width)],
                    gain_in.at[k - 1], s_g1.at[k - 1], r_g1.at[k - 1], {"dp": to},
                )
                copy.start()
                gain_copies.append(copy)
                copy = remote(cbuf.at[dp], cbuf.at[dp], s_c.at[k - 1], r_c.at[k - 1], {"dp": to})
                copy.start()
                c_copies.append(copy)
        for k in range(1, ns):
            block = gram.at[turn, from_at_s(k)]
            remote(
                block, block, s_gr.at[turn, k - 1], r_gr.at[turn, k - 1], {"section": at_s(k)}
            ).wait_recv()
        table = gram[turn, 0]
        for s in range(1, ns):
            table = table + gram[turn, s]
        table = eliminate(table + unit, 0, rank // 2, row_of)
        for copy in copies:
            copy.wait()
        own = pl.ds(pl.multiple_of(sec * slab, slab), slab)
        total = upart[turn, own, :]
        for k in range(1, ns):
            total = total + from_s[turn, k - 1]
        zsum[turn, dp] = total
        copies = []
        for k in range(1, nd):
            block = zsum.at[turn, dp]
            copy = remote(block, block, s_uz.at[turn, k - 1], r_uz.at[turn, k - 1], {"dp": at_z(k)})
            copy.start()
            copies.append(copy)
        sends += copies
        table = eliminate(table, rank // 2, rank, row_of)
        pivots = jnp.sum(jnp.where(lanes == sub_rows, table, 0.0), axis=2, keepdims=True)
        inverse = (table * (1.0 / jnp.sqrt(pivots)))[:, :, rank : 2 * rank]
        for k in range(1, nd):
            block = zsum.at[turn, from_at_z(k)]
            remote(block, block, s_uz.at[turn, k - 1], r_uz.at[turn, k - 1], {"dp": at_z(k)}).wait_recv()
        total = zsum[turn, 0]
        for d in range(1, nd):
            total = total + zsum[turn, d]
        ufull[turn, own, :] = total * (1.0 / nd)
        copies = []
        for k in range(1, ns):
            block = ufull.at[turn, own, :]
            copy = remote(block, block, s_ug.at[turn, k - 1], r_ug.at[turn, k - 1], {"section": at_s(k)})
            copy.start()
            copies.append(copy)
        sends += copies
        if turn == ROUNDS - 1:
            for j in range(2):
                a, b, c = pieces(exact(inverse[j], pfull[turn, j], NN))
                left_stack[j] = jnp.concatenate([a, a, b, b, a, c], axis=0)
        for k in range(1, ns):
            there = pl.ds(pl.multiple_of(from_at_s(k) * slab, slab), slab)
            block = ufull.at[turn, there, :]
            remote(block, block, s_ug.at[turn, k - 1], r_ug.at[turn, k - 1], {"section": at_s(k)}).wait_recv()
        factors = [exact(inverse[j], ufull[turn, pl.ds(j * rank, rank), :], NN) for j in range(2)]
        if turn == 0:
            gain_total = gain_grads[:, pl.ds(pl.multiple_of(dp * width, width), width)]
            for k in range(1, nd):
                gain_copies[k - 1].wait()
                gain_total = gain_total + gain_in[k - 1]
            new_gain_momentum = beta_decay * gain_momentum[...] + gain_total * (1.0 / nd)
            new_gain_master = gain_master[...] - step_rate * new_gain_momentum
            gmom_out[...] = new_gain_momentum
            gmaster_out[...] = new_gain_master
            gain_all[dp] = new_gain_master
            for k in range(1, nd):
                block = gain_all.at[dp]
                copy = remote(block, block, s_g2.at[k - 1], r_g2.at[k - 1], {"dp": at_z(k)})
                copy.start()
                sends.append(copy)

    for j in range(2):
        a, b, c = pieces(factors[j])
        right_stack[j] = jnp.concatenate([a, b, a, b, c, a], axis=0)

    def approx(j, start, size):
        return dot(left_stack[j, :, pl.ds(start, size)], right_stack[j], TN)

    for j in range(2):
        for first, size in ((early, late), (0, early)):
            part = approx(j, pl.multiple_of(dp * share + first, 128), size)
            at = pl.ds(first, size)
            new_momentum = beta_decay * mobuf[j, at, :] + part
            new_master = mabuf[j, at, :] - step_rate * new_momentum
            mobuf[j, at, :] = new_momentum
            mabuf[j, at, :] = new_master
            if first == early:
                wlate[j] = new_master.astype(BF16)
        if j == 1:
            pass
    there = w_out.at[:, pl.ds(pl.multiple_of(dp * share + early, 128), late), :]
    w_copies = []
    for k in range(1, nd):
        copy = remote(wlate, there, s_w.at[k - 1], r_w.at[k - 1], {"dp": at_z(k)})
        copy.start()
        w_copies.append(copy)
    outs = [
        pltpu.make_async_copy(wlate, there, out_sem.at[0]),
        pltpu.make_async_copy(mobuf, mom_out, out_sem.at[1]),
        pltpu.make_async_copy(mabuf, master_out, out_sem.at[2]),
    ]
    for copy in outs:
        copy.start()
    for k in range(nd):
        owner = from_at_z(k)
        if k:
            block = cbuf.at[owner]
            remote(block, block, s_c.at[k - 1], r_c.at[k - 1], {"dp": at_z(k)}).wait_recv()
            sends.append(c_copies[k - 1])
        for j in range(2):
            for first, size in ((0, early), (early, late)):
                start = pl.multiple_of(owner * share + first, 128)
                part = approx(j, start, size)
                at = pl.ds(start, size)
                ebuf[j, at, :] = ebuf[j, at, :] - part
                if first == 0:
                    wearly[owner, j] = (cbuf[owner, j] - step_rate * part).astype(BF16)
        whole = pl.ds(pl.multiple_of(owner * share, 128), share)
        head = pl.ds(pl.multiple_of(owner * share, 128), early)
        for copy in (
            pltpu.make_async_copy(ebuf.at[:, whole, :], err_out.at[:, whole, :], out_sem.at[3 + 2 * k]),
            pltpu.make_async_copy(wearly.at[owner], w_out.at[:, head, :], out_sem.at[4 + 2 * k]),
        ):
            copy.start()
            outs.append(copy)
    for k in range(1, nd):
        block = gain_all.at[from_at_z(k)]
        remote(block, block, s_g2.at[k - 1], r_g2.at[k - 1], {"dp": at_z(k)}).wait_recv()
    for d in range(nd):
        gains_out[:, d * width : (d + 1) * width] = gain_all[d].astype(BF16)
    for copy in sends:
        copy.wait_send()
    for copy in outs:
        copy.wait()
    for k in range(1, nd):
        w_copies[k - 1].wait_send()
        block = w_out.at[:, pl.ds(pl.multiple_of(from_at_z(k) * share + early, 128), late), :]
        remote(wlate, block, s_w.at[k - 1], r_w.at[k - 1], {"dp": at_z(k)}).wait_recv()


def local_fused(nd, ns, grads, errors, start_q, master, momentum, gain_grads, gain_master, gain_momentum):
    _, two, rows, cols = grads.shape
    rank = start_q.shape[1]
    share, piece, slab = rows // nd, rank // nd, 2 * rank // ns
    early = share // 2
    width = gain_master.shape[1]
    hbm = pl.BlockSpec(memory_space=pl.ANY)
    vmem = pl.BlockSpec(memory_space=pltpu.VMEM)
    sem = pltpu.SemaphoreType.DMA
    turns = ROUNDS
    pair = lambda *shape: [sem(shape), sem(shape)]
    out = pl.pallas_call(
        functools.partial(kernel, nd, ns, early),
        out_shape=(
            jax.ShapeDtypeStruct((two, rows, cols), F32),
            jax.ShapeDtypeStruct((two, share, cols), F32),
            jax.ShapeDtypeStruct((two, share, cols), F32),
            jax.ShapeDtypeStruct((two, rows, cols), BF16),
            jax.ShapeDtypeStruct((two, width), F32),
            jax.ShapeDtypeStruct((two, width), F32),
            jax.ShapeDtypeStruct((two, width * nd), BF16),
        ),
        in_specs=[hbm, hbm, vmem, hbm, hbm, vmem, vmem, vmem],
        out_specs=(hbm, hbm, hbm, hbm, vmem, vmem, vmem),
        scratch_shapes=[
            pltpu.VMEM((two, rows, cols), BF16),
            pltpu.VMEM((two, rows, cols), F32),
            pltpu.VMEM((two, rows, cols), BF16),
            pltpu.VMEM((two, rows, cols), BF16),
            pltpu.VMEM((two, share, cols), F32),
            pltpu.VMEM((two, share, cols), F32),
            pltpu.VMEM((turns, two, rank, rows), F32),
            pltpu.VMEM((turns, rank, rows), F32),
            pltpu.VMEM((turns, rank, rows), F32),
            pltpu.VMEM((turns, nd - 1, piece, rows), F32),
            pltpu.VMEM((turns, two, rank, rows), F32),
            pltpu.VMEM((turns, ns, two, rank, 128), F32),
            pltpu.VMEM((turns, two * rank, cols), F32),
            pltpu.VMEM((turns, ns - 1, slab, cols), F32),
            pltpu.VMEM((turns, nd, slab, cols), F32),
            pltpu.VMEM((8, 128), F32),
            pltpu.VMEM((turns, two * rank, cols), F32),
            pltpu.VMEM((nd, two, early, cols), F32),
            pltpu.VMEM((nd, two, early, cols), BF16),
            pltpu.VMEM((two, share - early, cols), BF16),
            pltpu.VMEM((nd - 1, two, width), F32),
            pltpu.VMEM((nd, two, width), F32),
            pltpu.VMEM((two, 6 * rank, rows), BF16),
            pltpu.VMEM((two, 6 * rank, cols), BF16),
            sem((6,)),
            sem((3 + 2 * nd,)),
        ]
        + pair(turns)
        + pair(turns, nd - 1)
        + pair(turns, nd - 1)
        + pair(turns, nd)
        + pair(turns, ns - 1)
        + pair(turns, ns - 1)
        + pair(turns, nd - 1)
        + pair(turns, ns - 1)
        + pair(nd - 1)
        + pair(nd - 1)
        + pair(nd - 1)
        + pair(nd - 1),
        compiler_params=pltpu.CompilerParams(
            collective_id=0, has_side_effects=True, vmem_limit_bytes=48 * 1024 * 1024
        ),
    )(grads[0], errors[0], start_q, master[:, 0], momentum[:, 0], gain_grads[0], gain_master, gain_momentum)
    return (out[0][None], out[1][:, None], out[2][:, None]) + tuple(out[3:])


def solution(mesh):
    nd, ns = mesh.shape["dp"], mesh.shape["section"]

    def local(grads, errors, start_q, *rest):
        rank, rows = start_q.shape[1], grads.shape[2]
        fits = rank % (8 * nd) == 0 and (2 * rank) % (8 * ns) == 0 and rows % (256 * nd) == 0
        if fits and mesh.shape["tensor"] == 2 and rank == 32:
            return local_fused(nd, ns, grads, errors, start_q, *rest)
        return local_plain(grads, errors, start_q, *rest)

    return jax.shard_map(
        local,
        mesh=mesh,
        in_specs=(
            P("dp", None, "section", "tensor"),
            P("dp", None, "section", "tensor"),
            P(None, None, "tensor"),
            P(None, "section", "dp", "tensor"),
            P(None, "section", "dp", "tensor"),
            P("dp", None, None),
            P(None, "dp"),
            P(None, "dp"),
        ),
        out_specs=(
            P("dp", None, "section", "tensor"),
            P(None, "section", "dp", "tensor"),
            P(None, "section", "dp", "tensor"),
            P(None, "section", "tensor"),
            P(None, "dp"),
            P(None, "dp"),
            P(),
        ),
        check_vma=False,
    )
```

```python
import functools

import jax
import jax.numpy as jnp
from jax import lax
from jax.experimental import pallas as pl
from jax.experimental.pallas import tpu as pltpu
from jax.sharding import PartitionSpec as P

ROUNDS = 2


beta_decay = 0.9
step_rate = 0.25

MESH = pl.DeviceIdType.MESH
F32 = jnp.float32
BF16 = jnp.bfloat16
NN = (((1,), (0,)), ((), ()))
NT = (((1,), (1,)), ((), ()))
TN = (((0,), (0,)), ((), ()))


def local_plain(grads, errors, start_q, master, momentum, gain_grads, gain_master, gain_momentum):
    highest = lax.Precision.HIGHEST
    replicas = lax.axis_size("dp")
    merged = grads[0].astype(jnp.float32) + errors[0]
    right_factor = start_q
    for turn in range(ROUNDS):
        partial_left = jnp.einsum("jak,jrk->jra", merged, right_factor, precision=highest)
        reduce_summed = lax.psum(partial_left, ("dp", "tensor"))
        left_factor = reduce_summed / replicas
        gram_part = jnp.einsum("jra,jsa->jrs", left_factor, left_factor, precision=highest)
        gram = lax.psum(gram_part, "section")
        lower = jnp.linalg.cholesky(gram)
        left_hat = jax.vmap(
            lambda tri, rhs: jax.scipy.linalg.solve_triangular(tri, rhs, lower=True)
        )(lower, left_factor)
        partial_right = jnp.einsum("jak,jra->jrk", merged, left_hat, precision=highest)
        summed = lax.psum(partial_right, ("dp", "section"))
        right_factor = summed / replicas
    approx = jnp.einsum("jra,jrk->jak", left_hat, right_factor, precision=highest)
    new_errors = (merged - approx)[None]
    share_rows = approx.shape[1] // replicas
    row_start = lax.axis_index("dp") * share_rows
    share = lax.dynamic_slice_in_dim(approx, row_start, share_rows, 1)[:, None]
    new_momentum = beta_decay * momentum + share
    new_master = master - step_rate * new_momentum
    gain_sum_all = lax.psum(gain_grads[0], "dp")
    share_width = gain_sum_all.shape[1] // replicas
    gain_share = lax.dynamic_slice_in_dim(
        gain_sum_all, lax.axis_index("dp") * share_width, share_width, 1
    )
    gain_mean = gain_share / replicas
    new_gain_momentum = beta_decay * gain_momentum + gain_mean
    new_gain_master = gain_master - step_rate * new_gain_momentum
    gathered, gains = (
        lax.all_gather(new_master.astype(jnp.bfloat16), "dp", axis=2, tiled=True),
        lax.all_gather(new_gain_master.astype(jnp.bfloat16), "dp", axis=1, tiled=True),
    )
    weights = gathered.reshape(gathered.shape[0], gathered.shape[2], gathered.shape[3])
    return (
        new_errors,
        new_momentum,
        new_master,
        weights,
        new_gain_momentum,
        new_gain_master,
        gains,
    )


def pieces(x):
    high = x.astype(BF16)
    rest = x - high.astype(F32)
    mid = rest.astype(BF16)
    return high, mid, (rest - mid.astype(F32)).astype(BF16)


def dot(a, b, dims):
    return lax.dot_general(a, b, dims, preferred_element_type=F32)


def exact(a, b, dims):
    return lax.dot_general(a, b, dims, precision=lax.Precision.HIGHEST, preferred_element_type=F32)


def folded(by_high, by_low, rank):
    small = by_high[2 * rank :] + by_low[rank : 2 * rank]
    return by_high[:rank] + ((by_high[rank : 2 * rank] + by_low[:rank]) + small)


def eliminate(table, first, last, rows):
    for i in range(first, last):
        row = table[:, i : i + 1, :]
        column = table[:, :, i : i + 1]
        scaled = row * (1.0 / table[:, i : i + 1, i : i + 1])
        table = table - jnp.where(rows > i, column, 0.0) * scaled
    return table


def kernel(
    nd, ns, early,
    grads, errors, start_q, master, momentum, gain_grads, gain_master, gain_momentum,
    err_out, mom_out, master_out, w_out, gmom_out, gmaster_out, gains_out,
    gbuf, ebuf, mhi, mlo, mabuf, mobuf, qbuf, gg, gma, gmo,
    ppart, from_core, psum, from_z, pfull,
    gram, upart, from_s, zsum, fbuf, ufull,
    cbuf, wall, gain_in, gain_all, left_stack, right_stack,
    in_sem, out_sem, s_core, r_core, s_z, r_z, s_gz, r_gz, s_fw, r_fw,
    s_gr, r_gr, s_u, r_u, s_uz, r_uz, s_ug, r_ug, s_c, r_c, s_w, r_w, s_g1, r_g1, s_g2, r_g2,
):
    rank, rows = start_q.shape[1], errors.shape[1]
    share = rows // nd
    late = share - early
    piece = rank // nd
    slab = 2 * rank // ns
    width = gain_master.shape[1]
    dp, me, sec = lax.axis_index("dp"), lax.axis_index("tensor"), lax.axis_index("section")
    sib = 1 - me

    def at_z(k):
        return lax.rem(dp + k, nd)

    def from_at_z(k):
        return lax.rem(dp + nd - k, nd)

    def at_s(k):
        return lax.rem(sec + k, ns)

    def from_at_s(k):
        return lax.rem(sec + ns - k, ns)

    def remote(src, dst, send, recv, where):
        return pltpu.make_async_remote_copy(
            src_ref=src, dst_ref=dst, send_sem=send, recv_sem=recv, device_id=where, device_id_type=MESH
        )

    def load(j, slot):
        return (
            pltpu.make_async_copy(grads.at[j], gbuf.at[j], in_sem.at[2 * slot]),
            pltpu.make_async_copy(errors.at[j], ebuf.at[j], in_sem.at[2 * slot + 1]),
        )

    load_master = pltpu.make_async_copy(master, mabuf, in_sem.at[4])
    load_momentum = pltpu.make_async_copy(momentum, mobuf, in_sem.at[5])
    load_q = pltpu.make_async_copy(start_q, qbuf, in_sem.at[6])
    load_gains = [
        pltpu.make_async_copy(gain_grads, gg, in_sem.at[7]),
        pltpu.make_async_copy(gain_master, gma, in_sem.at[8]),
        pltpu.make_async_copy(gain_momentum, gmo, in_sem.at[9]),
    ]
    load_master.start()
    load_momentum.start()
    load_q.start()
    for slot, j in enumerate((sib, me)):
        for copy in load(j, slot):
            copy.start()
    for copy in load_gains:
        copy.start()

    barrier = pltpu.get_barrier_semaphore()
    pl.semaphore_signal(barrier, inc=1, device_id={"tensor": sib}, device_id_type=MESH)
    for k in range(1, nd):
        pl.semaphore_signal(barrier, inc=1, device_id={"dp": at_z(k)}, device_id_type=MESH)
    for k in range(1, ns):
        pl.semaphore_signal(barrier, inc=1, device_id={"section": at_s(k)}, device_id_type=MESH)

    sends = []

    def inside(z):
        return jnp.logical_and(z >= 0, z < nd)

    def hop(block_of, send, recv, step, side, start):
        owner, to = dp - side * (step - 1), dp + side

        @pl.when(jnp.logical_and(inside(owner), inside(to)))
        def _():
            block = block_of(lax.rem(owner + nd, nd))
            copy = remote(block, block, send, recv, {"dp": lax.rem(to + nd, nd)})
            if start:
                copy.start()
            else:
                copy.wait_send()

    def landed(block_of, send, recv, step, side):
        owner = dp - side * step

        @pl.when(inside(owner))
        def _():
            block = block_of(lax.rem(owner + nd, nd))
            remote(block, block, send, recv, {"dp": lax.rem(dp - side + nd, nd)}).wait_recv()

    def c_sems(step, side):
        return s_c.at[step - 1, (side + 1) // 2], r_c.at[step - 1, (side + 1) // 2]

    def c_step(step):
        for side in (1, -1):
            if 1 < step <= nd:
                landed(cbuf.at.__getitem__, *c_sems(step - 1, side), step - 1, side)
            if step < nd:
                hop(cbuf.at.__getitem__, *c_sems(step, side), step, side, True)

    def w_block(j):
        return lambda owner: wall.at[owner, j, pl.ds(early, late), :]

    def w_sems(step, side, j):
        return s_w.at[step - 1, (side + 1) // 2, j], r_w.at[step - 1, (side + 1) // 2, j]

    def w_step(step, j):
        for side in (1, -1):
            if step > 1:
                landed(w_block(j), *w_sems(step - 1, side, j), step - 1, side)
            if step < nd:
                hop(w_block(j), *w_sems(step, side, j), step, side, True)

    def prepare(j, slot):
        for copy in load(j, slot):
            copy.wait()
        stack = jnp.concatenate(pieces(qbuf[j]), axis=0)

        def chunk(i, carry):
            base = pl.multiple_of(i * 256, 256)
            for sub in range(4):
                at = pl.ds(pl.multiple_of(base + sub * 64, 64), 64)
                merged = gbuf[j, at, :].astype(F32) + ebuf[j, at, :]
                ebuf[j, at, :] = merged
                high = merged.astype(BF16)
                mhi[j, at, :] = high
                mlo[j, at, :] = (merged - high.astype(F32)).astype(BF16)
            at = pl.ds(base, 256)
            ppart[0, j, :, at] = folded(
                dot(stack, mhi[j, at, :], NT), dot(stack[: 2 * rank], mlo[j, at, :], NT), rank
            )
            return carry

        lax.fori_loop(0, rows // 256, chunk, 0)

    def left_part(turn, j, factor):
        stack = jnp.concatenate(pieces(factor), axis=0)
        ppart[turn, j] = folded(dot(stack, mhi[j], NT), dot(stack[: 2 * rank], mlo[j], NT), rank)

    lanes = lax.broadcasted_iota(jnp.int32, (2, rank, 128), 2)
    sub_rows = lax.broadcasted_iota(jnp.int32, (2, rank, 128), 1)
    unit = jnp.where(lanes == sub_rows + rank, 1.0, 0.0).astype(F32)
    row_of = lax.broadcasted_iota(jnp.int32, (2, rank, 1), 1)
    gain_copies = []
    load_master.wait()
    load_momentum.wait()
    for j in range(2):
        cbuf[dp, j] = mabuf[j, :early, :] - (step_rate * beta_decay) * mobuf[j, :early, :]
    pl.semaphore_wait(barrier, nd + ns - 1)
    c_step(1)
    load_q.wait()
    for turn in range(ROUNDS):
        if turn == 0:
            prepare(sib, 0)
        else:
            left_part(turn, sib, fbuf[sib])
        swap = remote(
            ppart.at[turn, sib], from_core.at[turn], s_core.at[turn], r_core.at[turn], {"tensor": sib}
        )
        swap.start()
        if turn == 0:
            prepare(me, 1)
        else:
            left_part(turn, me, fbuf[me])
        swap.wait()
        psum[turn] = ppart[turn, me] + from_core[turn]
        copies = []
        for k in range(1, nd):
            to = at_z(k)
            copy = remote(
                psum.at[turn, pl.ds(pl.multiple_of(to * piece, piece), piece), :],
                from_z.at[turn, k - 1],
                s_z.at[turn, k - 1],
                r_z.at[turn, k - 1],
                {"dp": to},
            )
            copy.start()
            copies.append(copy)
        mine = pl.ds(pl.multiple_of(dp * piece, piece), piece)
        for copy in copies:
            copy.wait()
        total = psum[turn, mine, :]
        for k in range(1, nd):
            total = total + from_z[turn, k - 1]
        pfull[turn, me, mine, :] = total * (1.0 / nd)
        own = pfull.at[turn, me, mine, :]
        gathers = []
        for k in range(1, nd):
            copy = remote(own, own, s_gz.at[turn, k - 1], r_gz.at[turn, k - 1], {"dp": at_z(k)})
            copy.start()
            gathers.append(copy)
        copy = remote(own, own, s_fw.at[turn, 0], r_fw.at[turn, 0], {"tensor": sib})
        copy.start()
        forwards = [copy]
        for k in range(1, nd):
            there = pl.ds(pl.multiple_of(from_at_z(k) * piece, piece), piece)
            block = pfull.at[turn, me, there, :]
            remote(block, block, s_gz.at[turn, k - 1], r_gz.at[turn, k - 1], {"dp": at_z(k)}).wait_recv()
            copy = remote(block, block, s_fw.at[turn, k], r_fw.at[turn, k], {"tensor": sib})
            copy.start()
            forwards.append(copy)
        for k in range(nd):
            there = pl.ds(pl.multiple_of(from_at_z(k) * piece, piece), piece)
            block = pfull.at[turn, sib, there, :]
            remote(block, block, s_fw.at[turn, k], r_fw.at[turn, k], {"tensor": sib}).wait_recv()
        sends += gathers + forwards
        if turn == 0:
            c_step(2)

        for j in range(2):
            left = pfull[turn, j]
            gram[turn, sec, j] = jnp.concatenate(
                [exact(left, left, NT), jnp.zeros((rank, 128 - rank), F32)], axis=1
            )
        grams = []
        for k in range(1, ns):
            copy = remote(
                gram.at[turn, sec], gram.at[turn, sec], s_gr.at[turn, k - 1], r_gr.at[turn, k - 1],
                {"section": at_s(k)},
            )
            copy.start()
            grams.append(copy)
        sends += grams
        for j in range(2):
            stack = jnp.concatenate(pieces(pfull[turn, j]), axis=0)
            upart[turn, pl.ds(j * rank, rank), :] = folded(
                dot(stack, mhi[j], NN), dot(stack[: 2 * rank], mlo[j], NN), rank
            )
        copies = []
        for k in range(1, ns):
            to = at_s(k)
            copy = remote(
                upart.at[turn, pl.ds(pl.multiple_of(to * slab, slab), slab), :],
                from_s.at[turn, k - 1],
                s_u.at[turn, k - 1],
                r_u.at[turn, k - 1],
                {"section": to},
            )
            copy.start()
            copies.append(copy)
        if turn == 0:
            for copy in load_gains:
                copy.wait()
            for k in range(1, nd):
                to = at_z(k)
                copy = remote(
                    gg.at[:, pl.ds(pl.multiple_of(to * width, width), width)],
                    gain_in.at[k - 1], s_g1.at[k - 1], r_g1.at[k - 1], {"dp": to},
                )
                copy.start()
                gain_copies.append(copy)
        for k in range(1, ns):
            block = gram.at[turn, from_at_s(k)]
            remote(
                block, block, s_gr.at[turn, k - 1], r_gr.at[turn, k - 1], {"section": at_s(k)}
            ).wait_recv()
        table = gram[turn, 0]
        for s in range(1, ns):
            table = table + gram[turn, s]
        table = eliminate(table + unit, 0, rank // 2, row_of)
        for copy in copies:
            copy.wait()
        own = pl.ds(pl.multiple_of(sec * slab, slab), slab)
        total = upart[turn, own, :]
        for k in range(1, ns):
            total = total + from_s[turn, k - 1]
        zsum[turn, dp] = total
        copies = []
        for k in range(1, nd):
            block = zsum.at[turn, dp]
            copy = remote(block, block, s_uz.at[turn, k - 1], r_uz.at[turn, k - 1], {"dp": at_z(k)})
            copy.start()
            copies.append(copy)
        sends += copies
        table = eliminate(table, rank // 2, rank, row_of)
        pivots = jnp.sum(jnp.where(lanes == sub_rows, table, 0.0), axis=2, keepdims=True)
        inverse = (table * (1.0 / jnp.sqrt(pivots)))[:, :, rank : 2 * rank]
        for k in range(1, nd):
            block = zsum.at[turn, from_at_z(k)]
            remote(block, block, s_uz.at[turn, k - 1], r_uz.at[turn, k - 1], {"dp": at_z(k)}).wait_recv()
        total = zsum[turn, 0]
        for d in range(1, nd):
            total = total + zsum[turn, d]
        ufull[turn, own, :] = total * (1.0 / nd)
        if turn == 0 and nd > 2:
            c_step(3)
        copies = []
        for k in range(1, ns):
            block = ufull.at[turn, own, :]
            copy = remote(block, block, s_ug.at[turn, k - 1], r_ug.at[turn, k - 1], {"section": at_s(k)})
            copy.start()
            copies.append(copy)
        sends += copies
        if turn == ROUNDS - 1:
            for j in range(2):
                a, b, c = pieces(exact(inverse[j], pfull[turn, j], NN))
                left_stack[j] = jnp.concatenate([a, a, b, b, a, c], axis=0)
        for k in range(1, ns):
            there = pl.ds(pl.multiple_of(from_at_s(k) * slab, slab), slab)
            block = ufull.at[turn, there, :]
            remote(block, block, s_ug.at[turn, k - 1], r_ug.at[turn, k - 1], {"section": at_s(k)}).wait_recv()
        for j in range(2):
            fbuf[j] = exact(inverse[j], ufull[turn, pl.ds(j * rank, rank), :], NN)
        if turn == 0:
            gain_total = gg[:, pl.ds(pl.multiple_of(dp * width, width), width)]
            for k in range(1, nd):
                gain_copies[k - 1].wait()
                gain_total = gain_total + gain_in[k - 1]
            new_gain_momentum = beta_decay * gmo[...] + gain_total * (1.0 / nd)
            new_gain_master = gma[...] - step_rate * new_gain_momentum
            gmom_out[...] = new_gain_momentum
            gmaster_out[...] = new_gain_master
            gain_all[dp] = new_gain_master
            for k in range(1, nd):
                block = gain_all.at[dp]
                copy = remote(block, block, s_g2.at[k - 1], r_g2.at[k - 1], {"dp": at_z(k)})
                copy.start()
                sends.append(copy)

    for j in range(2):
        a, b, c = pieces(fbuf[j])
        right_stack[j] = jnp.concatenate([a, b, a, b, c, a], axis=0)

    def approx(j, owner):
        at = pl.ds(pl.multiple_of(owner * share, share), share)
        part = dot(left_stack[j, :, at], right_stack[j], TN)
        return part, at

    outs = []

    def send_out(src, dst):
        copy = pltpu.make_async_copy(src, dst, out_sem.at[len(outs)])
        copy.start()
        outs.append(copy)

    for j in range(2):
        part, at = approx(j, dp)
        new_momentum = beta_decay * mobuf[j] + part
        new_master = mabuf[j] - step_rate * new_momentum
        mobuf[j] = new_momentum
        mabuf[j] = new_master
        wall[dp, j, early:, :] = new_master[early:].astype(BF16)
        w_step(1, j)
        ebuf[j, at, :] = ebuf[j, at, :] - part
        wall[dp, j, :early, :] = (cbuf[dp, j] - step_rate * part[:early]).astype(BF16)
    send_out(mobuf, mom_out)
    send_out(mabuf, master_out)
    if nd > 1:
        c_step(nd)
    for k in range(nd):
        owner = from_at_z(k)
        if k:
            for j in range(2):
                part, at = approx(j, owner)
                ebuf[j, at, :] = ebuf[j, at, :] - part
                wall[owner, j, :early, :] = (cbuf[owner, j] - step_rate * part[:early]).astype(BF16)
        whole = pl.ds(pl.multiple_of(owner * share, share), share)
        send_out(ebuf.at[:, whole, :], err_out.at[:, whole, :])
    for step in range(2, nd + 1):
        for j in range(2):
            w_step(step, j)
    for k in range(nd):
        owner = from_at_z(k)
        whole = pl.ds(pl.multiple_of(owner * share, share), share)
        send_out(wall.at[owner], w_out.at[:, whole, :])
    for k in range(1, nd):
        block = gain_all.at[from_at_z(k)]
        remote(block, block, s_g2.at[k - 1], r_g2.at[k - 1], {"dp": at_z(k)}).wait_recv()
    for d in range(nd):
        gains_out[:, d * width : (d + 1) * width] = gain_all[d].astype(BF16)
    for copy in sends:
        copy.wait_send()
    for step in range(1, nd):
        for side in (1, -1):
            hop(cbuf.at.__getitem__, *c_sems(step, side), step, side, False)
            for j in range(2):
                hop(w_block(j), *w_sems(step, side, j), step, side, False)
    for copy in outs:
        copy.wait()


def local_fused(nd, ns, grads, errors, start_q, master, momentum, gain_grads, gain_master, gain_momentum):
    _, two, rows, cols = grads.shape
    rank = start_q.shape[1]
    share, piece, slab = rows // nd, rank // nd, 2 * rank // ns
    early = share // 4
    width = gain_master.shape[1]
    hbm = pl.BlockSpec(memory_space=pltpu.MemorySpace.HBM)
    vmem = pl.BlockSpec(memory_space=pltpu.VMEM)
    sem = pltpu.SemaphoreType.DMA
    turns = ROUNDS
    pair = lambda *shape: [sem(shape), sem(shape)]
    out = pl.pallas_call(
        functools.partial(kernel, nd, ns, early),
        out_shape=(
            jax.ShapeDtypeStruct((two, rows, cols), F32),
            jax.ShapeDtypeStruct((two, share, cols), F32),
            jax.ShapeDtypeStruct((two, share, cols), F32),
            jax.ShapeDtypeStruct((two, rows, cols), BF16),
            jax.ShapeDtypeStruct((two, width), F32),
            jax.ShapeDtypeStruct((two, width), F32),
            jax.ShapeDtypeStruct((two, width * nd), BF16),
        ),
        in_specs=[hbm] * 8,
        out_specs=(hbm, hbm, hbm, hbm, vmem, vmem, vmem),
        scratch_shapes=[
            pltpu.VMEM((two, rows, cols), BF16),
            pltpu.VMEM((two, rows, cols), F32),
            pltpu.VMEM((two, rows, cols), BF16),
            pltpu.VMEM((two, rows, cols), BF16),
            pltpu.VMEM((two, share, cols), F32),
            pltpu.VMEM((two, share, cols), F32),
            pltpu.VMEM((two, rank, cols), F32),
            pltpu.VMEM((two, width * nd), F32),
            pltpu.VMEM((two, width), F32),
            pltpu.VMEM((two, width), F32),
            pltpu.VMEM((turns, two, rank, rows), F32),
            pltpu.VMEM((turns, rank, rows), F32),
            pltpu.VMEM((turns, rank, rows), F32),
            pltpu.VMEM((turns, nd - 1, piece, rows), F32),
            pltpu.VMEM((turns, two, rank, rows), F32),
            pltpu.VMEM((turns, ns, two, rank, 128), F32),
            pltpu.VMEM((turns, two * rank, cols), F32),
            pltpu.VMEM((turns, ns - 1, slab, cols), F32),
            pltpu.VMEM((turns, nd, slab, cols), F32),
            pltpu.VMEM((two, rank, cols), F32),
            pltpu.VMEM((turns, two * rank, cols), F32),
            pltpu.VMEM((nd, two, early, cols), F32),
            pltpu.VMEM((nd, two, share, cols), BF16),
            pltpu.VMEM((nd - 1, two, width), F32),
            pltpu.VMEM((nd, two, width), F32),
            pltpu.VMEM((two, 6 * rank, rows), BF16),
            pltpu.VMEM((two, 6 * rank, cols), BF16),
            sem((10,)),
            sem((2 + 2 * nd,)),
        ]
        + pair(turns)
        + pair(turns, nd - 1)
        + pair(turns, nd - 1)
        + pair(turns, nd)
        + pair(turns, ns - 1)
        + pair(turns, ns - 1)
        + pair(turns, nd - 1)
        + pair(turns, ns - 1)
        + pair(nd - 1, 2)
        + pair(nd - 1, 2, two)
        + pair(nd - 1)
        + pair(nd - 1),
        compiler_params=pltpu.CompilerParams(
            collective_id=0, has_side_effects=True, vmem_limit_bytes=48 * 1024 * 1024
        ),
    )(grads[0], errors[0], start_q, master[:, 0], momentum[:, 0], gain_grads[0], gain_master, gain_momentum)
    return (out[0][None], out[1][:, None], out[2][:, None]) + tuple(out[3:])


def solution(mesh):
    nd, ns = mesh.shape["dp"], mesh.shape["section"]

    def local(grads, errors, start_q, *rest):
        rank, rows = start_q.shape[1], grads.shape[2]
        fits = rank % (8 * nd) == 0 and (2 * rank) % (8 * ns) == 0 and rows % (256 * nd) == 0
        if fits and nd > 1 and mesh.shape["tensor"] == 2 and rank == 32:
            return local_fused(nd, ns, grads, errors, start_q, *rest)
        return local_plain(grads, errors, start_q, *rest)

    return jax.shard_map(
        local,
        mesh=mesh,
        in_specs=(
            P("dp", None, "section", "tensor"),
            P("dp", None, "section", "tensor"),
            P(None, None, "tensor"),
            P(None, "section", "dp", "tensor"),
            P(None, "section", "dp", "tensor"),
            P("dp", None, None),
            P(None, "dp"),
            P(None, "dp"),
        ),
        out_specs=(
            P("dp", None, "section", "tensor"),
            P(None, "section", "dp", "tensor"),
            P(None, "section", "dp", "tensor"),
            P(None, "section", "tensor"),
            P(None, "dp"),
            P(None, "dp"),
            P(),
        ),
        check_vma=False,
    )
```

```python
import functools

import jax
import jax.numpy as jnp
from jax import lax
from jax.experimental import pallas as pl
from jax.experimental.pallas import tpu as pltpu
from jax.sharding import PartitionSpec as P

ROUNDS = 2


beta_decay = 0.9
step_rate = 0.25

MESH = pl.DeviceIdType.MESH
F32 = jnp.float32
BF16 = jnp.bfloat16
NN = (((1,), (0,)), ((), ()))
NT = (((1,), (1,)), ((), ()))
TN = (((0,), (0,)), ((), ()))


def local_plain(grads, errors, start_q, master, momentum, gain_grads, gain_master, gain_momentum):
    highest = lax.Precision.HIGHEST
    replicas = lax.axis_size("dp")
    merged = grads[0].astype(jnp.float32) + errors[0]
    right_factor = start_q
    for turn in range(ROUNDS):
        partial_left = jnp.einsum("jak,jrk->jra", merged, right_factor, precision=highest)
        reduce_summed = lax.psum(partial_left, ("dp", "tensor"))
        left_factor = reduce_summed / replicas
        gram_part = jnp.einsum("jra,jsa->jrs", left_factor, left_factor, precision=highest)
        gram = lax.psum(gram_part, "section")
        lower = jnp.linalg.cholesky(gram)
        left_hat = jax.vmap(
            lambda tri, rhs: jax.scipy.linalg.solve_triangular(tri, rhs, lower=True)
        )(lower, left_factor)
        partial_right = jnp.einsum("jak,jra->jrk", merged, left_hat, precision=highest)
        summed = lax.psum(partial_right, ("dp", "section"))
        right_factor = summed / replicas
    approx = jnp.einsum("jra,jrk->jak", left_hat, right_factor, precision=highest)
    new_errors = (merged - approx)[None]
    share_rows = approx.shape[1] // replicas
    row_start = lax.axis_index("dp") * share_rows
    share = lax.dynamic_slice_in_dim(approx, row_start, share_rows, 1)[:, None]
    new_momentum = beta_decay * momentum + share
    new_master = master - step_rate * new_momentum
    gain_sum_all = lax.psum(gain_grads[0], "dp")
    share_width = gain_sum_all.shape[1] // replicas
    gain_share = lax.dynamic_slice_in_dim(
        gain_sum_all, lax.axis_index("dp") * share_width, share_width, 1
    )
    gain_mean = gain_share / replicas
    new_gain_momentum = beta_decay * gain_momentum + gain_mean
    new_gain_master = gain_master - step_rate * new_gain_momentum
    gathered, gains = (
        lax.all_gather(new_master.astype(jnp.bfloat16), "dp", axis=2, tiled=True),
        lax.all_gather(new_gain_master.astype(jnp.bfloat16), "dp", axis=1, tiled=True),
    )
    weights = gathered.reshape(gathered.shape[0], gathered.shape[2], gathered.shape[3])
    return (
        new_errors,
        new_momentum,
        new_master,
        weights,
        new_gain_momentum,
        new_gain_master,
        gains,
    )


def pieces(x):
    high = x.astype(BF16)
    rest = x - high.astype(F32)
    mid = rest.astype(BF16)
    return high, mid, (rest - mid.astype(F32)).astype(BF16)


def dot(a, b, dims):
    return lax.dot_general(a, b, dims, preferred_element_type=F32)


def exact(a, b, dims):
    return lax.dot_general(a, b, dims, precision=lax.Precision.HIGHEST, preferred_element_type=F32)


def folded(by_high, by_low, rank):
    small = by_high[2 * rank :] + by_low[rank : 2 * rank]
    return by_high[:rank] + ((by_high[rank : 2 * rank] + by_low[:rank]) + small)


def eliminate(table, first, last, rows):
    for i in range(first, last):
        row = table[:, i : i + 1, :]
        column = table[:, :, i : i + 1]
        scaled = row * (1.0 / table[:, i : i + 1, i : i + 1])
        table = table - jnp.where(rows > i, column, 0.0) * scaled
    return table


def kernel(
    nd, ns, early,
    grads, errors, start_q, master, momentum, gain_grads, gain_master, gain_momentum,
    err_out, mom_out, master_out, w_out, gmom_out, gmaster_out, gains_out,
    gbuf, ebuf, mhi, mlo, mabuf, mobuf, qbuf, gg, gma, gmo,
    ppart, from_core, psum, from_z, pfull,
    gram, upart, from_s, zsum, fbuf, ufull,
    cbuf, wall, gain_in, gain_all, left_stack, right_stack,
    in_sem, out_sem, s_core, r_core, s_z, r_z, s_gz, r_gz, s_fw, r_fw,
    s_gr, r_gr, s_u, r_u, s_uz, r_uz, s_ug, r_ug, s_c, r_c, s_w, r_w, s_g1, r_g1, s_g2, r_g2,
):
    rank, rows = start_q.shape[1], errors.shape[1]
    share = rows // nd
    late = share - early
    piece = rank // nd
    slab = 2 * rank // ns
    width = gain_master.shape[1]
    dp, me, sec = lax.axis_index("dp"), lax.axis_index("tensor"), lax.axis_index("section")
    sib = 1 - me

    def at_z(k):
        return lax.rem(dp + k, nd)

    def from_at_z(k):
        return lax.rem(dp + nd - k, nd)

    def at_s(k):
        return lax.rem(sec + k, ns)

    def from_at_s(k):
        return lax.rem(sec + ns - k, ns)

    def remote(src, dst, send, recv, where):
        return pltpu.make_async_remote_copy(
            src_ref=src, dst_ref=dst, send_sem=send, recv_sem=recv, device_id=where, device_id_type=MESH
        )

    def load(j, slot):
        return (
            pltpu.make_async_copy(grads.at[j], gbuf.at[j], in_sem.at[2 * slot]),
            pltpu.make_async_copy(errors.at[j], ebuf.at[j], in_sem.at[2 * slot + 1]),
        )

    load_master = pltpu.make_async_copy(master, mabuf, in_sem.at[4])
    load_momentum = pltpu.make_async_copy(momentum, mobuf, in_sem.at[5])
    load_q = pltpu.make_async_copy(start_q, qbuf, in_sem.at[6])
    load_gains = [
        pltpu.make_async_copy(gain_grads, gg, in_sem.at[7]),
        pltpu.make_async_copy(gain_master, gma, in_sem.at[8]),
        pltpu.make_async_copy(gain_momentum, gmo, in_sem.at[9]),
    ]
    load_master.start()
    load_momentum.start()
    load_q.start()
    for slot, j in enumerate((sib, me)):
        for copy in load(j, slot):
            copy.start()
    for copy in load_gains:
        copy.start()

    barrier = pltpu.get_barrier_semaphore()
    pl.semaphore_signal(barrier, inc=1, device_id={"tensor": sib}, device_id_type=MESH)
    for k in range(1, nd):
        pl.semaphore_signal(barrier, inc=1, device_id={"dp": at_z(k)}, device_id_type=MESH)
    for k in range(1, ns):
        pl.semaphore_signal(barrier, inc=1, device_id={"section": at_s(k)}, device_id_type=MESH)

    sends = []

    def inside(z):
        return jnp.logical_and(z >= 0, z < nd)

    def hop(block_of, send, recv, step, side, start):
        owner, to = dp - side * (step - 1), dp + side

        @pl.when(jnp.logical_and(inside(owner), inside(to)))
        def _():
            block = block_of(lax.rem(owner + nd, nd))
            copy = remote(block, block, send, recv, {"dp": lax.rem(to + nd, nd)})
            if start:
                copy.start()
            else:
                copy.wait_send()

    def landed(block_of, send, recv, step, side):
        owner = dp - side * step

        @pl.when(inside(owner))
        def _():
            block = block_of(lax.rem(owner + nd, nd))
            remote(block, block, send, recv, {"dp": lax.rem(dp - side + nd, nd)}).wait_recv()

    def c_sems(step, side):
        return s_c.at[step - 1, (side + 1) // 2], r_c.at[step - 1, (side + 1) // 2]

    def c_step(step):
        for side in (1, -1):
            if 1 < step <= nd:
                landed(cbuf.at.__getitem__, *c_sems(step - 1, side), step - 1, side)
            if step < nd:
                hop(cbuf.at.__getitem__, *c_sems(step, side), step, side, True)

    def w_block(j):
        return lambda owner: wall.at[owner, j, pl.ds(early, late), :]

    def w_sems(step, side, j):
        return s_w.at[step - 1, (side + 1) // 2, j], r_w.at[step - 1, (side + 1) // 2, j]

    def w_step(step, j):
        for side in (1, -1):
            if step > 1:
                landed(w_block(j), *w_sems(step - 1, side, j), step - 1, side)
            if step < nd:
                hop(w_block(j), *w_sems(step, side, j), step, side, True)

    def prepare(j, slot):
        for copy in load(j, slot):
            copy.wait()
        stack = jnp.concatenate(pieces(qbuf[j]), axis=0)

        def chunk(i, carry):
            base = pl.multiple_of(i * 256, 256)
            for sub in range(4):
                at = pl.ds(pl.multiple_of(base + sub * 64, 64), 64)
                merged = gbuf[j, at, :].astype(F32) + ebuf[j, at, :]
                ebuf[j, at, :] = merged
                high = merged.astype(BF16)
                mhi[j, at, :] = high
                mlo[j, at, :] = (merged - high.astype(F32)).astype(BF16)
            at = pl.ds(base, 256)
            ppart[0, j, :, at] = folded(
                dot(stack, mhi[j, at, :], NT), dot(stack[: 2 * rank], mlo[j, at, :], NT), rank
            )
            return carry

        lax.fori_loop(0, rows // 256, chunk, 0)

    def left_part(turn, j, factor):
        stack = jnp.concatenate(pieces(factor), axis=0)
        ppart[turn, j] = folded(dot(stack, mhi[j], NT), dot(stack[: 2 * rank], mlo[j], NT), rank)

    lanes = lax.broadcasted_iota(jnp.int32, (2, rank, 128), 2)
    sub_rows = lax.broadcasted_iota(jnp.int32, (2, rank, 128), 1)
    unit = jnp.where(lanes == sub_rows + rank, 1.0, 0.0).astype(F32)
    row_of = lax.broadcasted_iota(jnp.int32, (2, rank, 1), 1)
    gain_copies = []
    load_master.wait()
    load_momentum.wait()
    for j in range(2):
        cbuf[dp, j] = mabuf[j, :early, :] - (step_rate * beta_decay) * mobuf[j, :early, :]
    pl.semaphore_wait(barrier, nd + ns - 1)
    c_step(1)
    load_q.wait()
    for turn in range(ROUNDS):
        if turn == 0:
            prepare(sib, 0)
        else:
            left_part(turn, sib, fbuf[sib])
        swap = remote(
            ppart.at[turn, sib], from_core.at[turn], s_core.at[turn], r_core.at[turn], {"tensor": sib}
        )
        swap.start()
        if turn == 0:
            prepare(me, 1)
        else:
            left_part(turn, me, fbuf[me])
        swap.wait()
        psum[turn] = ppart[turn, me] + from_core[turn]
        copies = []
        for k in range(1, nd):
            to = at_z(k)
            copy = remote(
                psum.at[turn, pl.ds(pl.multiple_of(to * piece, piece), piece), :],
                from_z.at[turn, k - 1],
                s_z.at[turn, k - 1],
                r_z.at[turn, k - 1],
                {"dp": to},
            )
            copy.start()
            copies.append(copy)
        mine = pl.ds(pl.multiple_of(dp * piece, piece), piece)
        for copy in copies:
            copy.wait()
        total = psum[turn, mine, :]
        for k in range(1, nd):
            total = total + from_z[turn, k - 1]
        pfull[turn, me, mine, :] = total * (1.0 / nd)
        own = pfull.at[turn, me, mine, :]
        gathers = []
        for k in range(1, nd):
            copy = remote(own, own, s_gz.at[turn, k - 1], r_gz.at[turn, k - 1], {"dp": at_z(k)})
            copy.start()
            gathers.append(copy)
        copy = remote(own, own, s_fw.at[turn, 0], r_fw.at[turn, 0], {"tensor": sib})
        copy.start()
        forwards = [copy]
        for k in range(1, nd):
            there = pl.ds(pl.multiple_of(from_at_z(k) * piece, piece), piece)
            block = pfull.at[turn, me, there, :]
            remote(block, block, s_gz.at[turn, k - 1], r_gz.at[turn, k - 1], {"dp": at_z(k)}).wait_recv()
            copy = remote(block, block, s_fw.at[turn, k], r_fw.at[turn, k], {"tensor": sib})
            copy.start()
            forwards.append(copy)
        for k in range(nd):
            there = pl.ds(pl.multiple_of(from_at_z(k) * piece, piece), piece)
            block = pfull.at[turn, sib, there, :]
            remote(block, block, s_fw.at[turn, k], r_fw.at[turn, k], {"tensor": sib}).wait_recv()
        sends += gathers + forwards
        if turn == 0:
            c_step(2)

        for j in range(2):
            left = pfull[turn, j]
            gram[turn, sec, j] = jnp.concatenate(
                [exact(left, left, NT), jnp.zeros((rank, 128 - rank), F32)], axis=1
            )
        grams = []
        for k in range(1, ns):
            copy = remote(
                gram.at[turn, sec], gram.at[turn, sec], s_gr.at[turn, k - 1], r_gr.at[turn, k - 1],
                {"section": at_s(k)},
            )
            copy.start()
            grams.append(copy)
        sends += grams
        for j in range(2):
            stack = jnp.concatenate(pieces(pfull[turn, j]), axis=0)
            upart[turn, pl.ds(j * rank, rank), :] = folded(
                dot(stack, mhi[j], NN), dot(stack[: 2 * rank], mlo[j], NN), rank
            )
        copies = []
        for k in range(1, ns):
            to = at_s(k)
            copy = remote(
                upart.at[turn, pl.ds(pl.multiple_of(to * slab, slab), slab), :],
                from_s.at[turn, k - 1],
                s_u.at[turn, k - 1],
                r_u.at[turn, k - 1],
                {"section": to},
            )
            copy.start()
            copies.append(copy)
        if turn == 0:
            for copy in load_gains:
                copy.wait()
            for k in range(1, nd):
                to = at_z(k)
                copy = remote(
                    gg.at[:, pl.ds(pl.multiple_of(to * width, width), width)],
                    gain_in.at[k - 1], s_g1.at[k - 1], r_g1.at[k - 1], {"dp": to},
                )
                copy.start()
                gain_copies.append(copy)
        for k in range(1, ns):
            block = gram.at[turn, from_at_s(k)]
            remote(
                block, block, s_gr.at[turn, k - 1], r_gr.at[turn, k - 1], {"section": at_s(k)}
            ).wait_recv()
        table = gram[turn, 0]
        for s in range(1, ns):
            table = table + gram[turn, s]
        table = eliminate(table + unit, 0, rank // 2, row_of)
        for copy in copies:
            copy.wait()
        own = pl.ds(pl.multiple_of(sec * slab, slab), slab)
        total = upart[turn, own, :]
        for k in range(1, ns):
            total = total + from_s[turn, k - 1]
        zsum[turn, dp] = total
        copies = []
        for k in range(1, nd):
            block = zsum.at[turn, dp]
            copy = remote(block, block, s_uz.at[turn, k - 1], r_uz.at[turn, k - 1], {"dp": at_z(k)})
            copy.start()
            copies.append(copy)
        sends += copies
        table = eliminate(table, rank // 2, rank, row_of)
        pivots = jnp.sum(jnp.where(lanes == sub_rows, table, 0.0), axis=2, keepdims=True)
        inverse = (table * (1.0 / jnp.sqrt(pivots)))[:, :, rank : 2 * rank]
        for k in range(1, nd):
            block = zsum.at[turn, from_at_z(k)]
            remote(block, block, s_uz.at[turn, k - 1], r_uz.at[turn, k - 1], {"dp": at_z(k)}).wait_recv()
        total = zsum[turn, 0]
        for d in range(1, nd):
            total = total + zsum[turn, d]
        ufull[turn, own, :] = total * (1.0 / nd)
        if turn == 0 and nd > 2:
            c_step(3)
        copies = []
        for k in range(1, ns):
            block = ufull.at[turn, own, :]
            copy = remote(block, block, s_ug.at[turn, k - 1], r_ug.at[turn, k - 1], {"section": at_s(k)})
            copy.start()
            copies.append(copy)
        sends += copies
        if turn == ROUNDS - 1:
            for j in range(2):
                a, b, c = pieces(exact(inverse[j], pfull[turn, j], NN))
                left_stack[j] = jnp.concatenate([a, a, b, b, a, c], axis=0)
        for k in range(1, ns):
            there = pl.ds(pl.multiple_of(from_at_s(k) * slab, slab), slab)
            block = ufull.at[turn, there, :]
            remote(block, block, s_ug.at[turn, k - 1], r_ug.at[turn, k - 1], {"section": at_s(k)}).wait_recv()
        for j in range(2):
            fbuf[j] = exact(inverse[j], ufull[turn, pl.ds(j * rank, rank), :], NN)
        if turn == 0:
            gain_total = gg[:, pl.ds(pl.multiple_of(dp * width, width), width)]
            for k in range(1, nd):
                gain_copies[k - 1].wait()
                gain_total = gain_total + gain_in[k - 1]
            new_gain_momentum = beta_decay * gmo[...] + gain_total * (1.0 / nd)
            new_gain_master = gma[...] - step_rate * new_gain_momentum
            gmom_out[...] = new_gain_momentum
            gmaster_out[...] = new_gain_master
            gain_all[dp] = new_gain_master
            for k in range(1, nd):
                block = gain_all.at[dp]
                copy = remote(block, block, s_g2.at[k - 1], r_g2.at[k - 1], {"dp": at_z(k)})
                copy.start()
                sends.append(copy)

    for j in range(2):
        a, b, c = pieces(fbuf[j])
        right_stack[j] = jnp.concatenate([a, b, a, b, c, a], axis=0)

    def approx(j, owner):
        at = pl.ds(pl.multiple_of(owner * share, share), share)
        part = dot(left_stack[j, :, at], right_stack[j], TN)
        return part, at

    outs = []

    def send_out(src, dst):
        copy = pltpu.make_async_copy(src, dst, out_sem.at[len(outs)])
        copy.start()
        outs.append(copy)

    for j in range(2):
        part, at = approx(j, dp)
        new_momentum = beta_decay * mobuf[j] + part
        new_master = mabuf[j] - step_rate * new_momentum
        mobuf[j] = new_momentum
        mabuf[j] = new_master
        wall[dp, j, early:, :] = new_master[early:].astype(BF16)
        w_step(1, j)
        ebuf[j, at, :] = ebuf[j, at, :] - part
        wall[dp, j, :early, :] = (cbuf[dp, j] - step_rate * part[:early]).astype(BF16)
    send_out(mobuf, mom_out)
    send_out(mabuf, master_out)
    if nd > 1:
        c_step(nd)
    for k in range(nd):
        owner = from_at_z(k)
        if k:
            for j in range(2):
                part, at = approx(j, owner)
                ebuf[j, at, :] = ebuf[j, at, :] - part
                wall[owner, j, :early, :] = (cbuf[owner, j] - step_rate * part[:early]).astype(BF16)
        whole = pl.ds(pl.multiple_of(owner * share, share), share)
        send_out(ebuf.at[:, whole, :], err_out.at[:, whole, :])
    for step in range(2, nd + 1):
        for j in range(2):
            w_step(step, j)
    for k in range(nd):
        owner = from_at_z(k)
        whole = pl.ds(pl.multiple_of(owner * share, share), share)
        send_out(wall.at[owner], w_out.at[:, whole, :])
    for k in range(1, nd):
        block = gain_all.at[from_at_z(k)]
        remote(block, block, s_g2.at[k - 1], r_g2.at[k - 1], {"dp": at_z(k)}).wait_recv()
    for d in range(nd):
        gains_out[:, d * width : (d + 1) * width] = gain_all[d].astype(BF16)
    for copy in sends:
        copy.wait_send()
    for step in range(1, nd):
        for side in (1, -1):
            hop(cbuf.at.__getitem__, *c_sems(step, side), step, side, False)
            for j in range(2):
                hop(w_block(j), *w_sems(step, side, j), step, side, False)
    for copy in outs:
        copy.wait()


def local_fused(nd, ns, grads, errors, start_q, master, momentum, gain_grads, gain_master, gain_momentum):
    _, two, rows, cols = grads.shape
    rank = start_q.shape[1]
    share, piece, slab = rows // nd, rank // nd, 2 * rank // ns
    early = share // 4
    width = gain_master.shape[1]
    hbm = pl.BlockSpec(memory_space=pltpu.MemorySpace.HBM)
    vmem = pl.BlockSpec(memory_space=pltpu.VMEM)
    sem = pltpu.SemaphoreType.DMA
    turns = ROUNDS
    pair = lambda *shape: [sem(shape), sem(shape)]
    out = pl.pallas_call(
        functools.partial(kernel, nd, ns, early),
        out_shape=(
            jax.ShapeDtypeStruct((two, rows, cols), F32),
            jax.ShapeDtypeStruct((two, share, cols), F32),
            jax.ShapeDtypeStruct((two, share, cols), F32),
            jax.ShapeDtypeStruct((two, rows, cols), BF16),
            jax.ShapeDtypeStruct((two, width), F32),
            jax.ShapeDtypeStruct((two, width), F32),
            jax.ShapeDtypeStruct((two, width * nd), BF16),
        ),
        in_specs=[hbm] * 8,
        out_specs=(hbm, hbm, hbm, hbm, vmem, vmem, vmem),
        scratch_shapes=[
            pltpu.VMEM((two, rows, cols), BF16),
            pltpu.VMEM((two, rows, cols), F32),
            pltpu.VMEM((two, rows, cols), BF16),
            pltpu.VMEM((two, rows, cols), BF16),
            pltpu.VMEM((two, share, cols), F32),
            pltpu.VMEM((two, share, cols), F32),
            pltpu.VMEM((two, rank, cols), F32),
            pltpu.VMEM((two, width * nd), F32),
            pltpu.VMEM((two, width), F32),
            pltpu.VMEM((two, width), F32),
            pltpu.VMEM((turns, two, rank, rows), F32),
            pltpu.VMEM((turns, rank, rows), F32),
            pltpu.VMEM((turns, rank, rows), F32),
            pltpu.VMEM((turns, nd - 1, piece, rows), F32),
            pltpu.VMEM((turns, two, rank, rows), F32),
            pltpu.VMEM((turns, ns, two, rank, 128), F32),
            pltpu.VMEM((turns, two * rank, cols), F32),
            pltpu.VMEM((turns, ns - 1, slab, cols), F32),
            pltpu.VMEM((turns, nd, slab, cols), F32),
            pltpu.VMEM((two, rank, cols), F32),
            pltpu.VMEM((turns, two * rank, cols), F32),
            pltpu.VMEM((nd, two, early, cols), F32),
            pltpu.VMEM((nd, two, share, cols), BF16),
            pltpu.VMEM((nd - 1, two, width), F32),
            pltpu.VMEM((nd, two, width), F32),
            pltpu.VMEM((two, 6 * rank, rows), BF16),
            pltpu.VMEM((two, 6 * rank, cols), BF16),
            sem((10,)),
            sem((2 + 2 * nd,)),
        ]
        + pair(turns)
        + pair(turns, nd - 1)
        + pair(turns, nd - 1)
        + pair(turns, nd)
        + pair(turns, ns - 1)
        + pair(turns, ns - 1)
        + pair(turns, nd - 1)
        + pair(turns, ns - 1)
        + pair(nd - 1, 2)
        + pair(nd - 1, 2, two)
        + pair(nd - 1)
        + pair(nd - 1),
        compiler_params=pltpu.CompilerParams(
            collective_id=0, has_side_effects=True, vmem_limit_bytes=63 * 1024 * 1024
        ),
    )(grads[0], errors[0], start_q, master[:, 0], momentum[:, 0], gain_grads[0], gain_master, gain_momentum)
    return (out[0][None], out[1][:, None], out[2][:, None]) + tuple(out[3:])


def solution(mesh):
    nd, ns = mesh.shape["dp"], mesh.shape["section"]

    def local(grads, errors, start_q, *rest):
        rank, rows = start_q.shape[1], grads.shape[2]
        fits = rank % (8 * nd) == 0 and (2 * rank) % (8 * ns) == 0 and rows % (256 * nd) == 0
        if fits and nd > 1 and mesh.shape["tensor"] == 2 and rank == 32:
            return local_fused(nd, ns, grads, errors, start_q, *rest)
        return local_plain(grads, errors, start_q, *rest)

    return jax.shard_map(
        local,
        mesh=mesh,
        in_specs=(
            P("dp", None, "section", "tensor"),
            P("dp", None, "section", "tensor"),
            P(None, None, "tensor"),
            P(None, "section", "dp", "tensor"),
            P(None, "section", "dp", "tensor"),
            P("dp", None, None),
            P(None, "dp"),
            P(None, "dp"),
        ),
        out_specs=(
            P("dp", None, "section", "tensor"),
            P(None, "section", "dp", "tensor"),
            P(None, "section", "dp", "tensor"),
            P(None, "section", "tensor"),
            P(None, "dp"),
            P(None, "dp"),
            P(),
        ),
        check_vma=False,
    )
```
